256 devices in a mesh: slab: 64 (over x_lo, y, z), subj: 2 (over core), tm: 2 (over x_hi).
Axes of the slice: x: 4 (x_hi: 2, x_lo: 2; x = x_hi * 2 + x_lo), y: 4, z: 8, core: 2. Of those that a mesh axis runs over, the one named last changes fastest.
Arguments:
- subject_data: bfloat16 [2, 128, 128, 2048], P('subj', 'slab', None, 'tm'), may hold values from -8 to 8
- template: bfloat16 [128, 128, 2048], P('slab', None, 'tm'), may hold values from -8 to 8
- neighbours: int32 [128, 27], P('slab'), may hold values from 0 to 127, as said below
- valid: int32 [128, 27], P('slab'), may hold values from 0 to 1, as said below
Outputs:
- new_template: bfloat16 [128, 128, 2048], P('slab', None, 'tm')
The draws below stay inside these ranges and needn't reach their ends.
Inputs may be any that keep to these rules, and one draw needn't show every extreme that they name: `neighbours`: slots 9 l to 9 l + 8 of block b name blocks of the slab of b shifted by l - 1 (slabs hold 2 consecutive blocks); where that slab doesn't exist they name b itself. Slot 13 names b itself. `valid`: slot 13 is always 1; slots whose slab doesn't exist are 0.
All inputs are finite; a program needn't handle non-finite values.
Results may differ from the reference program's by a relative error of at most 0.007.
Values may be sent and summed in bfloat16 or wider, within the bound.
A program may use at most 64 MiB of HBM per device.

```python
import jax
import jax.numpy as jnp
from jax import lax

VB = 128
NB = 27
TIMES = 2048
ITERS = 3
BLK_DEV = 2
BLOCKS = 128
SUBJECTS = 2


def base_signal(key):
    signal_key = jax.random.fold_in(key, 11)
    return jax.random.normal(signal_key, (BLOCKS, VB, TIMES), jnp.float32)


def draw_template(key, part):
    signal = base_signal(key)
    return jnp.clip(signal, -8.0, 8.0).astype(jnp.bfloat16)


def draw_subject_data(key, part):
    signal = base_signal(key)[None]
    strength = jax.random.uniform(jax.random.fold_in(key, 12), (1, BLOCKS, VB, 1), jnp.float32, 0.05, 0.3)
    noise_key = jax.random.fold_in(key, 14)
    shape = (SUBJECTS, BLOCKS, VB, TIMES)
    noise = jax.random.normal(noise_key, shape, jnp.float32)
    mixed = strength * signal + jnp.sqrt(1.0 - strength * strength) * noise
    return jnp.clip(mixed, -8.0, 8.0).astype(jnp.bfloat16)


def neighbour_table(key):
    blocks = jnp.arange(BLOCKS, dtype=jnp.int32)[:, None]
    slot = jnp.arange(NB, dtype=jnp.int32)[None, :]
    slabs = BLOCKS // BLK_DEV
    target = blocks // BLK_DEV + slot // (NB // 3) - 1
    offset = jax.random.randint(jax.random.fold_in(key, 21), (BLOCKS, NB), 0, BLK_DEV, dtype=jnp.int32)
    present = (target >= 0) & (target < slabs)
    centre = slot == NB // 2
    named = jnp.where(present, target * BLK_DEV + offset, blocks)
    named = jnp.where(centre, blocks, named)
    keep = jax.random.randint(jax.random.fold_in(key, 22), (BLOCKS, NB), 0, 4, dtype=jnp.int32) > 0
    flag = jnp.where(centre, 1, jnp.where(present & keep, 1, 0))
    return (named.astype(jnp.int32), flag.astype(jnp.int32))


def draw_neighbours(key, part):
    return neighbour_table(key)[0]


def draw_valid(key, part):
    return neighbour_table(key)[1]


def setup_inputs(seed: int = 0) -> dict:
    key_of = jax.random.split(jax.random.key(seed), 5)
    return {
        "subject_data": draw_subject_data(jax.random.fold_in(key_of[4], 71), 0),
        "template": draw_template(jax.random.fold_in(key_of[4], 71), 0),
        "neighbours": draw_neighbours(jax.random.fold_in(key_of[4], 71), 0),
        "valid": draw_valid(jax.random.fold_in(key_of[4], 71), 0),
    }


def balance(cross, row_norm, col_norm, mask):
    width = cross.shape[-1]
    logits = cross * row_norm[None, :, None, None] * col_norm[:, None, :, :] / 0.03
    masked = mask[None, None, :, None]
    kernel = jnp.exp(logits) * masked
    target = masked / (width * jnp.sum(mask))
    filler = 1.0 - masked
    col_weight = jnp.ones((cross.shape[0], 1, cross.shape[2], width), jnp.float32)
    for step in range(ITERS):
        row_weight = 1.0 / width / lax.optimization_barrier(jnp.sum(kernel * col_weight, axis=(2, 3), keepdims=True))
        col_weight = target / (lax.optimization_barrier(jnp.sum(kernel * row_weight, axis=1, keepdims=True)) + filler)
    flow = kernel * col_weight
    return (flow / lax.optimization_barrier(jnp.sum(flow, axis=(2, 3), keepdims=True))).astype(jnp.bfloat16)

def reference(subject_data, template, neighbours, valid):
    high = lax.Precision.HIGHEST
    tmpl = template.astype(jnp.float32)
    row_scale = lax.rsqrt(lax.optimization_barrier(jnp.sum(tmpl * tmpl, axis=-1)) + 1e-06)
    data = subject_data.astype(jnp.float32)
    col_scale = lax.rsqrt(lax.optimization_barrier(jnp.sum(data * data, axis=-1)) + 1e-06)

    def one_block(index):
        slots = neighbours[index].astype(jnp.int32)
        mask = valid[index].astype(jnp.float32)
        near = jnp.take(subject_data, slots, axis=1).astype(jnp.float32)
        cross = jnp.einsum('it,skjt->sikj', tmpl[index], near, precision=high)
        plan = balance(cross, row_scale[index], jnp.take(col_scale, slots, axis=1), mask)
        moved = jnp.einsum('sikj,skjt->it', plan.astype(jnp.float32), near, precision=high)
        return (moved / SUBJECTS).astype(jnp.bfloat16)
    return lax.map(one_block, jnp.arange(BLOCKS, dtype=jnp.int32))
```

```python
import jax
import jax.numpy as jnp
from jax import lax
from jax.experimental import pallas as pl
from jax.experimental.pallas import tpu as pltpu
from jax.sharding import PartitionSpec as P

MESH = pl.DeviceIdType.MESH
ITERS = 3
SCALE = 32760.0
TINY = 1e-6
PIECES = 4
OUT_PIECES = 4


def times_transposed(a, b):
    return lax.dot_general(a, b, (((1,), (1,)), ((), ())), preferred_element_type=jnp.float32)


def body(
    data_ref, tmpl_ref, near_ref, valid_ref, mine_ref, theirs_ref,
    ext, tmpl, part, code_out, code_in, norm_out, norm_in, kern, plan, moved,
    local_sem, slab_send, slab_recv, code_send, code_recv, norm_send, norm_recv, subj_send, subj_recv, mine_sem,
):
    slab, slabs = lax.axis_index("slab"), lax.axis_size("slab")
    subj, half = lax.axis_index("subj"), lax.axis_index("tm")
    rows, times = data_ref.shape
    width = 128
    blocks = rows // width
    piece = rows // PIECES
    tiles = blocks + PIECES
    has_prev, has_next = slab > 0, slab < slabs - 1

    copies = [
        pltpu.make_async_copy(tmpl_ref, tmpl, local_sem.at[0]),
        pltpu.make_async_copy(data_ref, ext.at[pl.ds(0, rows)], local_sem.at[1]),
    ]
    for copy in copies:
        copy.start()

    barrier = pltpu.get_barrier_semaphore()

    def greet(where):
        pl.semaphore_signal(barrier, inc=1, device_id=where, device_id_type=MESH)

    greet({"subj": 1 - subj})
    greet({"tm": 1 - half})

    @pl.when(has_prev)
    def _():
        greet({"slab": slab - 1})

    @pl.when(has_next)
    def _():
        greet({"slab": slab + 1})

    @pl.when(has_prev & has_next)
    def _():
        pl.semaphore_wait(barrier, 4)

    @pl.when(jnp.logical_not(has_prev & has_next))
    def _():
        pl.semaphore_wait(barrier, 3)

    def slab_copy(q, up):
        place = blocks * width + q * 2 * piece + (0 if up else piece)
        k = q + (0 if up else PIECES)
        return pltpu.make_async_remote_copy(
            src_ref=data_ref.at[pl.ds(q * piece, piece)],
            dst_ref=ext.at[pl.ds(place, piece)],
            send_sem=slab_send.at[k],
            recv_sem=slab_recv.at[k],
            device_id={"slab": slab + 1 if up else slab - 1},
            device_id_type=MESH,
        )

    for q in range(PIECES):

        @pl.when(has_next)
        def _():
            slab_copy(q, True).start()

        @pl.when(has_prev)
        def _():
            slab_copy(q, False).start()

    @pl.when(jnp.logical_not(has_prev))
    def _():
        for q in range(PIECES):
            ext[pl.ds(blocks * width + q * 2 * piece, piece), :] = jnp.zeros((piece, times), ext.dtype)

    @pl.when(jnp.logical_not(has_next))
    def _():
        for q in range(PIECES):
            ext[pl.ds(blocks * width + q * 2 * piece + piece, piece), :] = jnp.zeros((piece, times), ext.dtype)

    seen = near_ref[...] - (slab - 1) * blocks
    used = valid_ref[...].astype(jnp.float32)
    count = [
        jnp.sum(jnp.where(seen == e, used, 0.0), axis=1, keepdims=True) for e in range(3 * blocks)
    ]
    goal = 1.0 / (width * jnp.sum(used, axis=1, keepdims=True))
    lane = lax.broadcasted_iota(jnp.int32, (1, width), 1)

    def counts(b, tile):
        if tile < blocks:
            return jnp.broadcast_to(count[blocks + tile][b : b + 1], (1, width))
        owner = (tile - blocks) * piece // width
        return jnp.where(lane < piece, count[owner][b : b + 1], count[2 * blocks + owner][b : b + 1])

    eye = lax.broadcasted_iota(jnp.int32, (width, width), 0) == lax.broadcasted_iota(
        jnp.int32, (width, width), 1
    )

    def diagonal(gram, axis):
        return jnp.sum(jnp.where(eye, gram, 0.0), axis=axis, keepdims=True)

    copies[0].wait()
    grams = [
        times_transposed(tmpl[pl.ds(b * width, width), :], tmpl[pl.ds(b * width, width), :])
        for b in range(blocks)
    ]
    row_sq = [diagonal(gram, 1) for gram in grams]
    row_unit = [lax.rsqrt(sq + TINY) * SCALE for sq in row_sq]

    def code_copy(tile):
        return pltpu.make_async_remote_copy(
            src_ref=code_out.at[tile], dst_ref=code_in.at[tile],
            send_sem=code_send.at[tile], recv_sem=code_recv.at[tile],
            device_id={"tm": 1 - half}, device_id_type=MESH,
        )

    def norm_copy(tile):
        return pltpu.make_async_remote_copy(
            src_ref=norm_out.at[tile], dst_ref=norm_in.at[tile],
            send_sem=norm_send.at[tile], recv_sem=norm_recv.at[tile],
            device_id={"tm": 1 - half}, device_id_type=MESH,
        )

    def first_pass(tile):
        data = ext[pl.ds(tile * width, width), :]
        col_sq = diagonal(times_transposed(data, data), 0)
        norm_out[tile] = jnp.concatenate(
            [col_sq] + [diagonal(gram, 0) for gram in grams] + [jnp.zeros((8 - 1 - blocks, width), jnp.float32)], axis=0
        )
        norm_copy(tile).start()
        col_unit = lax.rsqrt(col_sq + TINY)
        for b in range(blocks):
            at = pl.ds(b * width, width)
            cross = times_transposed(tmpl[at, :], data)
            part[tile, at, :] = cross
            code_out[tile, at, :] = jnp.round(cross * row_unit[b] * col_unit).astype(jnp.int32).astype(jnp.int16)
        code_copy(tile).start()

    scales = {}

    def second_pass(tile):
        norm_copy(tile).wait_recv()
        there = norm_in[tile]
        if tile == 0:
            for b in range(blocks):
                other = jnp.sum(jnp.where(eye, there[1 + b : 2 + b], 0.0), axis=1, keepdims=True)
                row_scale = lax.rsqrt(row_sq[b] + other + 1e-6)
                scales[b] = (row_scale, row_scale * ((other + TINY) * lax.rsqrt(other + TINY)))
        col_sq = norm_out[tile][0:1]
        other = there[0:1]
        col_scale = lax.rsqrt(col_sq + other + 1e-6) * (1.0 / 0.03)
        col_other = col_scale * ((other + TINY) * lax.rsqrt(other + TINY)) * (1.0 / SCALE)
        code_copy(tile).wait_recv()
        for b in range(blocks):
            at = pl.ds(b * width, width)
            logits = part[tile, at, :] * (scales[b][0] * col_scale)
            logits += code_in[tile, at, :].astype(jnp.int32).astype(jnp.float32) * (scales[b][1] * col_other)
            kern[tile, at, :] = jnp.exp(logits)

    def arrived(q):
        @pl.when(has_prev)
        def _():
            slab_copy(q, True).wait_recv()

        @pl.when(has_next)
        def _():
            slab_copy(q, False).wait_recv()

    copies[1].wait()
    for tile in range(blocks):
        first_pass(tile)
    behind = 0
    for q in range(PIECES):
        arrived(q)
        first_pass(blocks + q)
        while behind < blocks + q:
            second_pass(behind)
            behind += 1
    while behind < tiles:
        second_pass(behind)
        behind += 1

    for b in range(blocks):
        at = pl.ds(b * width, width)
        number = [counts(b, tile) for tile in range(tiles)]
        weight = number
        for _ in range(ITERS):
            total = sum(kern[tile, at, :] * weight[tile] for tile in range(tiles))
            row_weight = (1.0 / width) / jnp.sum(total, axis=1, keepdims=True)
            weight = [
                number[tile] * goal[b : b + 1] / jnp.sum(kern[tile, at, :] * row_weight, axis=0, keepdims=True)
                for tile in range(tiles)
            ]
        total = sum(kern[tile, at, :] * weight[tile] for tile in range(tiles))
        share = 0.5 / jnp.sum(total, axis=1, keepdims=True)
        for tile in range(tiles):
            plan[at, pl.ds(tile * width, width)] = (kern[tile, at, :] * weight[tile] * share).astype(plan.dtype)

    wide = times // OUT_PIECES
    moves = []
    for c in range(OUT_PIECES):
        at = (slice(None), pl.ds(c * wide, wide))
        moved[at] = jnp.dot(plan[...], ext[at], preferred_element_type=jnp.float32).astype(moved.dtype)
        moves.append(
            pltpu.make_async_remote_copy(
                src_ref=moved.at[at], dst_ref=theirs_ref.at[at],
                send_sem=subj_send.at[c], recv_sem=subj_recv.at[c],
                device_id={"subj": 1 - subj}, device_id_type=MESH,
            )
        )
        moves.append(pltpu.make_async_copy(moved.at[at], mine_ref.at[at], mine_sem.at[c]))
        for move in moves[-2:]:
            move.start()

    for tile in range(tiles):
        norm_copy(tile).wait_send()
        code_copy(tile).wait_send()
    for q in range(PIECES):

        @pl.when(has_next)
        def _():
            slab_copy(q, True).wait_send()

        @pl.when(has_prev)
        def _():
            slab_copy(q, False).wait_send()

    for move in moves:
        move.wait()


def on_device(subject_data, template, neighbours, valid):
    _, blocks, width, times = subject_data.shape
    rows = blocks * width
    tiles = blocks + PIECES
    dma = pltpu.SemaphoreType.DMA
    anywhere = pl.BlockSpec(memory_space=pl.ANY)
    vmem = pl.BlockSpec(memory_space=pltpu.VMEM)
    mine, theirs = pl.pallas_call(
        body,
        out_shape=[jax.ShapeDtypeStruct((rows, times), jnp.bfloat16)] * 2,
        in_specs=[anywhere, anywhere, vmem, vmem],
        out_specs=[anywhere, anywhere],
        scratch_shapes=[
            pltpu.VMEM((tiles * width, times), jnp.bfloat16),
            pltpu.VMEM((rows, times), jnp.bfloat16),
            pltpu.VMEM((tiles, rows, width), jnp.float32),
            pltpu.VMEM((tiles, rows, width), jnp.int16),
            pltpu.VMEM((tiles, rows, width), jnp.int16),
            pltpu.VMEM((tiles, 8, width), jnp.float32),
            pltpu.VMEM((tiles, 8, width), jnp.float32),
            pltpu.VMEM((tiles, rows, width), jnp.float32),
            pltpu.VMEM((rows, tiles * width), jnp.bfloat16),
            pltpu.VMEM((rows, times), jnp.bfloat16),
            dma((2,)),
            dma((2 * PIECES,)), dma((2 * PIECES,)),
            dma((tiles,)), dma((tiles,)),
            dma((tiles,)), dma((tiles,)),
            dma((OUT_PIECES,)), dma((OUT_PIECES,)), dma((OUT_PIECES,)),
        ],
        compiler_params=pltpu.CompilerParams(
            collective_id=0, has_side_effects=True, vmem_limit_bytes=32 * 2**20
        ),
    )(subject_data.reshape(rows, times), template.reshape(rows, times), neighbours, valid)
    total = mine.astype(jnp.float32) + theirs.astype(jnp.float32)
    return total.astype(jnp.bfloat16).reshape(template.shape)


def solution(mesh):
    placed = (
        P("subj", "slab", None, "tm"),
        P("slab", None, "tm"),
        P("slab", None),
        P("slab", None),
    )
    return jax.shard_map(
        on_device, mesh=mesh, in_specs=placed, out_specs=P("slab", None, "tm"), check_vma=False
    )
```

```python
import jax
import jax.numpy as jnp
from jax import lax
from jax.experimental import pallas as pl
from jax.experimental.pallas import tpu as pltpu
from jax.sharding import PartitionSpec as P

MESH = pl.DeviceIdType.MESH
ITERS = 3
SCALE = 32760.0
TINY = 1e-6
PIECES = 4
PASSED = (2, 3)
OUT_PIECES = 4


def times_transposed(a, b):
    return lax.dot_general(a, b, (((1,), (1,)), ((), ())), preferred_element_type=jnp.float32)


def body(
    data_ref, tmpl_ref, near_ref, valid_ref, mine_ref, theirs_ref,
    ext, tmpl, near, valid, relayed, part, code_out, code_in, norm_out, norm_in, kern, plan,
    local_sem, slab_send, slab_recv, pass_send, pass_recv, code_send, code_recv, norm_send, norm_recv, subj_send, subj_recv,
):
    slab, slabs = lax.axis_index("slab"), lax.axis_size("slab")
    subj, half = lax.axis_index("subj"), lax.axis_index("tm")
    rows, times = data_ref.shape
    width = 128
    blocks = rows // width
    piece = rows // PIECES
    tiles = blocks + PIECES
    last, low, high = slabs - 1, slabs // 2 - 1, slabs // 2
    has_prev, has_next = slab > 0, slab < last
    at_edge, at_middle = (slab == 0) | (slab == last), (slab == low) | (slab == high)

    copies = [
        pltpu.make_async_copy(tmpl_ref, tmpl, local_sem.at[0]),
        pltpu.make_async_copy(data_ref, ext.at[pl.ds(0, rows)], local_sem.at[1]),
        pltpu.make_async_copy(near_ref, near, local_sem.at[2]),
        pltpu.make_async_copy(valid_ref, valid, local_sem.at[3]),
    ]
    for copy in copies:
        copy.start()

    barrier = pltpu.get_barrier_semaphore()

    def greet(where):
        pl.semaphore_signal(barrier, inc=1, device_id=where, device_id_type=MESH)

    greet({"subj": 1 - subj})
    greet({"tm": 1 - half})

    @pl.when(has_prev)
    def _():
        greet({"slab": slab - 1})

    @pl.when(has_next)
    def _():
        greet({"slab": slab + 1})

    @pl.when(at_edge)
    def _():
        greet({"slab": low})
        greet({"slab": high})
        pl.semaphore_wait(barrier, 5)

    @pl.when(at_middle)
    def _():
        greet({"slab": 0})
        greet({"slab": last})
        pl.semaphore_wait(barrier, 6)

    @pl.when(jnp.logical_not(at_edge | at_middle))
    def _():
        pl.semaphore_wait(barrier, 4)

    def slab_place(q, up):
        return ext.at[pl.ds(blocks * width + q * 2 * piece + (0 if up else piece), piece)]

    def slab_copy(q, up):
        k = q + (0 if up else PIECES)
        return pltpu.make_async_remote_copy(
            src_ref=data_ref.at[pl.ds(q * piece, piece)],
            dst_ref=slab_place(q, up),
            send_sem=slab_send.at[k],
            recv_sem=slab_recv.at[k],
            device_id={"slab": slab + 1 if up else slab - 1},
            device_id_type=MESH,
        )

    def pass_copy(q, up):
        k = 0 if up else 1
        return pltpu.make_async_remote_copy(
            src_ref=data_ref.at[pl.ds(q * piece, piece)],
            dst_ref=relayed.at[k],
            send_sem=slab_send.at[q + (0 if up else PIECES)],
            recv_sem=pass_recv.at[k],
            device_id={"slab": 0 if q == PASSED[0] else last},
            device_id_type=MESH,
        )

    for q in PASSED:
        for up, here in ((True, low), (False, high)):

            @pl.when(slab == here)
            def _():
                pass_copy(q, up).start()

    for q in range(PIECES):

        @pl.when(has_next & (slab != low) if q in PASSED else has_next)
        def _():
            slab_copy(q, True).start()

        @pl.when(has_prev & (slab != high) if q in PASSED else has_prev)
        def _():
            slab_copy(q, False).start()

    def onward(q, up):
        return pltpu.make_async_remote_copy(
            src_ref=relayed.at[0 if up else 1],
            dst_ref=slab_place(q, up),
            send_sem=pass_send.at[0 if up else 1],
            recv_sem=slab_recv.at[q + (0 if up else PIECES)],
            device_id={"slab": high if up else low},
            device_id_type=MESH,
        )

    def pass_on(act):
        for q, here in zip(PASSED, (0, last)):

            @pl.when(slab == here)
            def _():
                for up in (True, False):
                    act(q, up)

    def pass_start(q, up):
        pass_copy(q, up).wait_recv()
        onward(q, up).start()

    @pl.when(jnp.logical_not(has_prev))
    def _():
        for q in range(PIECES):
            ext[pl.ds(blocks * width + q * 2 * piece, piece), :] = jnp.zeros((piece, times), ext.dtype)

    @pl.when(jnp.logical_not(has_next))
    def _():
        for q in range(PIECES):
            ext[pl.ds(blocks * width + q * 2 * piece + piece, piece), :] = jnp.zeros((piece, times), ext.dtype)

    copies[2].wait()
    copies[3].wait()
    seen = near[...] - (slab - 1) * blocks
    used = valid[...].astype(jnp.float32)
    count = [
        jnp.sum(jnp.where(seen == e, used, 0.0), axis=1, keepdims=True) for e in range(3 * blocks)
    ]
    goal = 1.0 / (width * jnp.sum(used, axis=1, keepdims=True))
    lane = lax.broadcasted_iota(jnp.int32, (1, width), 1)

    def counts(b, tile):
        if tile < blocks:
            return jnp.broadcast_to(count[blocks + tile][b : b + 1], (1, width))
        owner = (tile - blocks) * piece // width
        return jnp.where(lane < piece, count[owner][b : b + 1], count[2 * blocks + owner][b : b + 1])

    eye = lax.broadcasted_iota(jnp.int32, (width, width), 0) == lax.broadcasted_iota(
        jnp.int32, (width, width), 1
    )

    def diagonal(gram, axis):
        return jnp.sum(jnp.where(eye, gram, 0.0), axis=axis, keepdims=True)

    copies[0].wait()
    grams = [
        times_transposed(tmpl[pl.ds(b * width, width), :], tmpl[pl.ds(b * width, width), :])
        for b in range(blocks)
    ]
    row_sq = [diagonal(gram, 1) for gram in grams]
    row_unit = [lax.rsqrt(sq + TINY) * SCALE for sq in row_sq]

    def code_copy(tile):
        return pltpu.make_async_remote_copy(
            src_ref=code_out.at[tile], dst_ref=code_in.at[tile],
            send_sem=code_send.at[tile], recv_sem=code_recv.at[tile],
            device_id={"tm": 1 - half}, device_id_type=MESH,
        )

    def norm_copy(tile):
        return pltpu.make_async_remote_copy(
            src_ref=norm_out.at[tile], dst_ref=norm_in.at[tile],
            send_sem=norm_send.at[tile], recv_sem=norm_recv.at[tile],
            device_id={"tm": 1 - half}, device_id_type=MESH,
        )

    def first_pass(tile):
        data = ext[pl.ds(tile * width, width), :]
        col_sq = diagonal(times_transposed(data, data), 0)
        norm_out[tile] = jnp.concatenate(
            [col_sq] + [diagonal(gram, 0) for gram in grams] + [jnp.zeros((8 - 1 - blocks, width), jnp.float32)], axis=0
        )
        norm_copy(tile).start()
        col_unit = lax.rsqrt(col_sq + TINY)
        for b in range(blocks):
            at = pl.ds(b * width, width)
            cross = times_transposed(tmpl[at, :], data)
            part[tile, at, :] = cross
            code_out[tile, at, :] = jnp.round(cross * row_unit[b] * col_unit).astype(jnp.int32).astype(jnp.int16)
        code_copy(tile).start()

    scales = {}

    def second_pass(tile):
        norm_copy(tile).wait_recv()
        there = norm_in[tile]
        if tile == 0:
            for b in range(blocks):
                other = jnp.sum(jnp.where(eye, there[1 + b : 2 + b], 0.0), axis=1, keepdims=True)
                row_scale = lax.rsqrt(row_sq[b] + other + 1e-6)
                scales[b] = (row_scale, row_scale * ((other + TINY) * lax.rsqrt(other + TINY)))
        col_sq = norm_out[tile][0:1]
        other = there[0:1]
        col_scale = lax.rsqrt(col_sq + other + 1e-6) * (1.0 / 0.03)
        col_other = col_scale * ((other + TINY) * lax.rsqrt(other + TINY)) * (1.0 / SCALE)
        code_copy(tile).wait_recv()
        for b in range(blocks):
            at = pl.ds(b * width, width)
            logits = part[tile, at, :] * (scales[b][0] * col_scale)
            logits += code_in[tile, at, :].astype(jnp.int32).astype(jnp.float32) * (scales[b][1] * col_other)
            kern[tile, at, :] = jnp.exp(logits)

    def arrived(q):
        @pl.when(has_prev)
        def _():
            slab_copy(q, True).wait_recv()

        @pl.when(has_next)
        def _():
            slab_copy(q, False).wait_recv()

    copies[1].wait()
    for tile in range(blocks):
        first_pass(tile)
    behind = 0
    for q in range(PIECES):
        arrived(q)
        first_pass(blocks + q)
        if q == 0:
            pass_on(pass_start)
        while behind < blocks + q:
            second_pass(behind)
            behind += 1
    while behind < tiles:
        second_pass(behind)
        behind += 1

    for b in range(blocks):
        at = pl.ds(b * width, width)
        number = [counts(b, tile) for tile in range(tiles)]
        weight = number
        for _ in range(ITERS):
            total = sum(kern[tile, at, :] * weight[tile] for tile in range(tiles))
            row_weight = (1.0 / width) / jnp.sum(total, axis=1, keepdims=True)
            weight = [
                number[tile] * goal[b : b + 1] / jnp.sum(kern[tile, at, :] * row_weight, axis=0, keepdims=True)
                for tile in range(tiles)
            ]
        total = sum(kern[tile, at, :] * weight[tile] for tile in range(tiles))
        share = 0.5 / jnp.sum(total, axis=1, keepdims=True)
        for tile in range(tiles):
            plan[at, pl.ds(tile * width, width)] = (kern[tile, at, :] * weight[tile] * share).astype(plan.dtype)

    wide = times // OUT_PIECES
    moves = []
    for c in range(OUT_PIECES):
        at = (slice(None), pl.ds(c * wide, wide))
        mine_ref[at] = jnp.dot(plan[...], ext[at], preferred_element_type=jnp.float32).astype(mine_ref.dtype)
        moves.append(
            pltpu.make_async_remote_copy(
                src_ref=mine_ref.at[at], dst_ref=theirs_ref.at[at],
                send_sem=subj_send.at[c], recv_sem=subj_recv.at[c],
                device_id={"subj": 1 - subj}, device_id_type=MESH,
            )
        )
        moves[-1].start()

    pass_on(lambda q, up: onward(q, up).wait_send())
    for tile in range(tiles):
        norm_copy(tile).wait_send()
        code_copy(tile).wait_send()
    for q in range(PIECES):

        @pl.when(has_next)
        def _():
            slab_copy(q, True).wait_send()

        @pl.when(has_prev)
        def _():
            slab_copy(q, False).wait_send()

    for move in moves:
        move.wait()


def on_device(subject_data, template, neighbours, valid):
    _, blocks, width, times = subject_data.shape
    rows = blocks * width
    tiles = blocks + PIECES
    dma = pltpu.SemaphoreType.DMA
    hbm = pl.BlockSpec(memory_space=pltpu.HBM)
    vmem = pl.BlockSpec(memory_space=pltpu.VMEM)
    mine, theirs = pl.pallas_call(
        body,
        out_shape=[jax.ShapeDtypeStruct((rows, times), jnp.bfloat16)] * 2,
        in_specs=[hbm] * 4,
        out_specs=[vmem] * 2,
        scratch_shapes=[
            pltpu.VMEM((tiles * width, times), jnp.bfloat16),
            pltpu.VMEM((rows, times), jnp.bfloat16),
            pltpu.VMEM(neighbours.shape, neighbours.dtype),
            pltpu.VMEM(valid.shape, valid.dtype),
            pltpu.VMEM((2, rows // PIECES, times), jnp.bfloat16),
            pltpu.VMEM((tiles, rows, width), jnp.float32),
            pltpu.VMEM((tiles, rows, width), jnp.int16),
            pltpu.VMEM((tiles, rows, width), jnp.int16),
            pltpu.VMEM((tiles, 8, width), jnp.float32),
            pltpu.VMEM((tiles, 8, width), jnp.float32),
            pltpu.VMEM((tiles, rows, width), jnp.float32),
            pltpu.VMEM((rows, tiles * width), jnp.bfloat16),
            dma((4,)),
            dma((2 * PIECES,)), dma((2 * PIECES,)),
            dma((2,)), dma((2,)),
            dma((tiles,)), dma((tiles,)),
            dma((tiles,)), dma((tiles,)),
            dma((OUT_PIECES,)), dma((OUT_PIECES,)),
        ],
        compiler_params=pltpu.CompilerParams(
            collective_id=0, has_side_effects=True, vmem_limit_bytes=32 * 2**20
        ),
    )(*[pltpu.with_memory_space_constraint(x, pltpu.HBM) for x in (subject_data.reshape(rows, times), template.reshape(rows, times), neighbours, valid)])
    total = mine.astype(jnp.float32) + theirs.astype(jnp.float32)
    return total.astype(jnp.bfloat16).reshape(template.shape)


def solution(mesh):
    placed = (
        P("subj", "slab", None, "tm"),
        P("slab", None, "tm"),
        P("slab", None),
        P("slab", None),
    )
    return jax.shard_map(
        on_device, mesh=mesh, in_specs=placed, out_specs=P("slab", None, "tm"), check_vma=False
    )
```

```python
import jax
import jax.numpy as jnp
from jax import lax
from jax.experimental import pallas as pl
from jax.experimental.pallas import tpu as pltpu
from jax.sharding import PartitionSpec as P

MESH = pl.DeviceIdType.MESH
ITERS = 3
SCALE = 32760.0
TINY = 1e-6
PIECES = 4
RUN = 8
DETOUR = (0, 1)
OUT_PIECES = 4


def times_transposed(a, b):
    return lax.dot_general(a, b, (((1,), (1,)), ((), ())), preferred_element_type=jnp.float32)


def body(
    data_ref, tmpl_ref, near_ref, valid_ref, mine_ref, theirs_ref,
    ext, tmpl, near, valid, passing, part, code_out, code_in, norm_out, norm_in, kern, plan,
    local_sem, slab_send, slab_recv, pass_send, pass_recv, code_send, code_recv, norm_send, norm_recv, subj_send, subj_recv,
):
    slab, slabs = lax.axis_index("slab"), lax.axis_size("slab")
    subj, half = lax.axis_index("subj"), lax.axis_index("tm")
    rows, times = data_ref.shape
    width = 128
    blocks = rows // width
    piece = rows // PIECES
    tiles = blocks + PIECES
    has_prev, has_next = slab > 0, slab < slabs - 1
    shared = (slabs // 2 - RUN, slabs // 2 + RUN - 1)
    byway = (shared[0] - RUN, shared[1] + RUN)

    copies = [
        pltpu.make_async_copy(tmpl_ref, tmpl, local_sem.at[0]),
        pltpu.make_async_copy(data_ref, ext.at[pl.ds(0, rows)], local_sem.at[1]),
        pltpu.make_async_copy(near_ref, near, local_sem.at[2]),
        pltpu.make_async_copy(valid_ref, valid, local_sem.at[3]),
    ]
    for copy in copies:
        copy.start()

    barrier = pltpu.get_barrier_semaphore()

    def greet(where):
        pl.semaphore_signal(barrier, inc=1, device_id=where, device_id_type=MESH)

    greet({"subj": 1 - subj})
    greet({"tm": 1 - half})

    @pl.when(has_prev)
    def _():
        greet({"slab": slab - 1})

    @pl.when(has_next)
    def _():
        greet({"slab": slab + 1})

    for crowded, way in zip(shared, byway):

        @pl.when(slab == crowded)
        def _():
            greet({"slab": way, "tm": 1 - half})

        @pl.when(slab == way)
        def _():
            greet({"slab": crowded})

    is_shared = (slab == shared[0]) | (slab == shared[1])
    is_byway = (slab == byway[0]) | (slab == byway[1])

    @pl.when(has_prev & has_next & jnp.logical_not(is_shared | is_byway))
    def _():
        pl.semaphore_wait(barrier, 4)

    @pl.when(is_shared | is_byway)
    def _():
        pl.semaphore_wait(barrier, 5)

    @pl.when(jnp.logical_not(has_prev & has_next))
    def _():
        pl.semaphore_wait(barrier, 3)

    def slab_place(q, up):
        return ext.at[pl.ds(blocks * width + q * 2 * piece + (0 if up else piece), piece)]

    def slab_copy(q, up):
        k = q + (0 if up else PIECES)
        return pltpu.make_async_remote_copy(
            src_ref=data_ref.at[pl.ds(q * piece, piece)],
            dst_ref=slab_place(q, up),
            send_sem=slab_send.at[k],
            recv_sem=slab_recv.at[k],
            device_id={"slab": slab + 1 if up else slab - 1},
            device_id_type=MESH,
        )

    for q in range(PIECES):

        @pl.when(has_next)
        def _():
            slab_copy(q, True).start()

        @pl.when(has_prev)
        def _():
            slab_copy(q, False).start()

    @pl.when(jnp.logical_not(has_prev))
    def _():
        for q in range(PIECES):
            ext[pl.ds(blocks * width + q * 2 * piece, piece), :] = jnp.zeros((piece, times), ext.dtype)

    @pl.when(jnp.logical_not(has_next))
    def _():
        for q in range(PIECES):
            ext[pl.ds(blocks * width + q * 2 * piece + piece, piece), :] = jnp.zeros((piece, times), ext.dtype)

    copies[2].wait()
    copies[3].wait()
    seen = near[...] - (slab - 1) * blocks
    used = valid[...].astype(jnp.float32)
    count = [
        jnp.sum(jnp.where(seen == e, used, 0.0), axis=1, keepdims=True) for e in range(3 * blocks)
    ]
    goal = 1.0 / (width * jnp.sum(used, axis=1, keepdims=True))
    lane = lax.broadcasted_iota(jnp.int32, (1, width), 1)

    def counts(b, tile):
        if tile < blocks:
            return jnp.broadcast_to(count[blocks + tile][b : b + 1], (1, width))
        owner = (tile - blocks) * piece // width
        return jnp.where(lane < piece, count[owner][b : b + 1], count[2 * blocks + owner][b : b + 1])

    eye = lax.broadcasted_iota(jnp.int32, (width, width), 0) == lax.broadcasted_iota(
        jnp.int32, (width, width), 1
    )

    def diagonal(gram, axis):
        return jnp.sum(jnp.where(eye, gram, 0.0), axis=axis, keepdims=True)

    copies[0].wait()
    grams = [
        times_transposed(tmpl[pl.ds(b * width, width), :], tmpl[pl.ds(b * width, width), :])
        for b in range(blocks)
    ]
    row_sq = [diagonal(gram, 1) for gram in grams]
    row_unit = [lax.rsqrt(sq + TINY) * SCALE for sq in row_sq]

    def code_copy(tile):
        return pltpu.make_async_remote_copy(
            src_ref=code_out.at[tile], dst_ref=code_in.at[tile],
            send_sem=code_send.at[tile], recv_sem=code_recv.at[tile],
            device_id={"tm": 1 - half}, device_id_type=MESH,
        )

    def detour_copy(tile, way):
        return pltpu.make_async_remote_copy(
            src_ref=code_out.at[tile], dst_ref=passing.at[tile],
            send_sem=code_send.at[tile], recv_sem=pass_recv.at[tile],
            device_id={"slab": way}, device_id_type=MESH,
        )

    def onward_copy(tile, crowded):
        return pltpu.make_async_remote_copy(
            src_ref=passing.at[tile], dst_ref=code_in.at[tile],
            send_sem=pass_send.at[tile], recv_sem=code_recv.at[tile],
            device_id={"slab": crowded, "tm": 1 - half}, device_id_type=MESH,
        )

    def send_code(tile):
        if tile not in DETOUR:
            code_copy(tile).start()
            return

        @pl.when(jnp.logical_not(is_shared))
        def _():
            code_copy(tile).start()

        for crowded, way in zip(shared, byway):

            @pl.when(slab == crowded)
            def _():
                detour_copy(tile, way).start()

    def pass_on():
        for crowded, way in zip(shared, byway):

            @pl.when(slab == way)
            def _():
                for tile in DETOUR:
                    detour_copy(tile, way).wait_recv()
                    onward_copy(tile, crowded).start()

    def norm_copy(tile):
        return pltpu.make_async_remote_copy(
            src_ref=norm_out.at[tile], dst_ref=norm_in.at[tile],
            send_sem=norm_send.at[tile], recv_sem=norm_recv.at[tile],
            device_id={"tm": 1 - half}, device_id_type=MESH,
        )

    def first_pass(tile):
        data = ext[pl.ds(tile * width, width), :]
        col_sq = diagonal(times_transposed(data, data), 0)
        norm_out[tile] = jnp.concatenate(
            [col_sq] + [diagonal(gram, 0) for gram in grams] + [jnp.zeros((8 - 1 - blocks, width), jnp.float32)], axis=0
        )
        norm_copy(tile).start()
        col_unit = lax.rsqrt(col_sq + TINY)
        for b in range(blocks):
            at = pl.ds(b * width, width)
            cross = times_transposed(tmpl[at, :], data)
            part[tile, at, :] = cross
            code_out[tile, at, :] = jnp.round(cross * row_unit[b] * col_unit).astype(jnp.int32).astype(jnp.int16)
        send_code(tile)

    scales = {}

    def second_pass(tile):
        norm_copy(tile).wait_recv()
        there = norm_in[tile]
        if tile == 0:
            for b in range(blocks):
                other = jnp.sum(jnp.where(eye, there[1 + b : 2 + b], 0.0), axis=1, keepdims=True)
                row_scale = lax.rsqrt(row_sq[b] + other + 1e-6)
                scales[b] = (row_scale, row_scale * ((other + TINY) * lax.rsqrt(other + TINY)))
        col_sq = norm_out[tile][0:1]
        other = there[0:1]
        col_scale = lax.rsqrt(col_sq + other + 1e-6) * (1.0 / 0.03)
        col_other = col_scale * ((other + TINY) * lax.rsqrt(other + TINY)) * (1.0 / SCALE)
        code_copy(tile).wait_recv()
        for b in range(blocks):
            at = pl.ds(b * width, width)
            logits = part[tile, at, :] * (scales[b][0] * col_scale)
            logits += code_in[tile, at, :].astype(jnp.int32).astype(jnp.float32) * (scales[b][1] * col_other)
            kern[tile, at, :] = jnp.exp(logits)

    def arrived(q):
        @pl.when(has_prev)
        def _():
            slab_copy(q, True).wait_recv()

        @pl.when(has_next)
        def _():
            slab_copy(q, False).wait_recv()

    copies[1].wait()
    for tile in range(blocks):
        first_pass(tile)
    pass_on()
    behind = 0
    for q in range(PIECES):
        arrived(q)
        first_pass(blocks + q)
        while behind < blocks + q:
            second_pass(behind)
            behind += 1
    while behind < tiles:
        second_pass(behind)
        behind += 1

    for b in range(blocks):
        at = pl.ds(b * width, width)
        number = [counts(b, tile) for tile in range(tiles)]
        weight = number
        for _ in range(ITERS):
            total = sum(kern[tile, at, :] * weight[tile] for tile in range(tiles))
            row_weight = (1.0 / width) / jnp.sum(total, axis=1, keepdims=True)
            weight = [
                number[tile] * goal[b : b + 1] / jnp.sum(kern[tile, at, :] * row_weight, axis=0, keepdims=True)
                for tile in range(tiles)
            ]
        total = sum(kern[tile, at, :] * weight[tile] for tile in range(tiles))
        share = 0.5 / jnp.sum(total, axis=1, keepdims=True)
        for tile in range(tiles):
            plan[at, pl.ds(tile * width, width)] = (kern[tile, at, :] * weight[tile] * share).astype(plan.dtype)

    wide = times // OUT_PIECES
    moves = []
    for c in range(OUT_PIECES):
        at = (slice(None), pl.ds(c * wide, wide))
        mine_ref[at] = jnp.dot(plan[...], ext[at], preferred_element_type=jnp.float32).astype(mine_ref.dtype)
        moves.append(
            pltpu.make_async_remote_copy(
                src_ref=mine_ref.at[at], dst_ref=theirs_ref.at[at],
                send_sem=subj_send.at[c], recv_sem=subj_recv.at[c],
                device_id={"subj": 1 - subj}, device_id_type=MESH,
            )
        )
        moves[-1].start()

    @pl.when(is_byway)
    def _():
        for tile in DETOUR:
            onward_copy(tile, slab).wait_send()

    for tile in range(tiles):
        norm_copy(tile).wait_send()
        code_copy(tile).wait_send()
    for q in range(PIECES):

        @pl.when(has_next)
        def _():
            slab_copy(q, True).wait_send()

        @pl.when(has_prev)
        def _():
            slab_copy(q, False).wait_send()

    for move in moves:
        move.wait()


def on_device(subject_data, template, neighbours, valid):
    _, blocks, width, times = subject_data.shape
    rows = blocks * width
    tiles = blocks + PIECES
    dma = pltpu.SemaphoreType.DMA
    hbm = pl.BlockSpec(memory_space=pltpu.HBM)
    vmem = pl.BlockSpec(memory_space=pltpu.VMEM)
    mine, theirs = pl.pallas_call(
        body,
        out_shape=[jax.ShapeDtypeStruct((rows, times), jnp.bfloat16)] * 2,
        in_specs=[hbm] * 4,
        out_specs=[vmem] * 2,
        scratch_shapes=[
            pltpu.VMEM((tiles * width, times), jnp.bfloat16),
            pltpu.VMEM((rows, times), jnp.bfloat16),
            pltpu.VMEM(neighbours.shape, neighbours.dtype),
            pltpu.VMEM(valid.shape, valid.dtype),
            pltpu.VMEM((len(DETOUR), rows, width), jnp.int16),
            pltpu.VMEM((tiles, rows, width), jnp.float32),
            pltpu.VMEM((tiles, rows, width), jnp.int16),
            pltpu.VMEM((tiles, rows, width), jnp.int16),
            pltpu.VMEM((tiles, 8, width), jnp.float32),
            pltpu.VMEM((tiles, 8, width), jnp.float32),
            pltpu.VMEM((tiles, rows, width), jnp.float32),
            pltpu.VMEM((rows, tiles * width), jnp.bfloat16),
            dma((4,)),
            dma((2 * PIECES,)), dma((2 * PIECES,)),
            dma((len(DETOUR),)), dma((len(DETOUR),)),
            dma((tiles,)), dma((tiles,)),
            dma((tiles,)), dma((tiles,)),
            dma((OUT_PIECES,)), dma((OUT_PIECES,)),
        ],
        compiler_params=pltpu.CompilerParams(
            collective_id=0, has_side_effects=True, vmem_limit_bytes=32 * 2**20
        ),
    )(*[pltpu.with_memory_space_constraint(x, pltpu.HBM) for x in (subject_data.reshape(rows, times), template.reshape(rows, times), neighbours, valid)])
    total = mine.astype(jnp.float32) + theirs.astype(jnp.float32)
    return total.astype(jnp.bfloat16).reshape(template.shape)


def solution(mesh):
    placed = (
        P("subj", "slab", None, "tm"),
        P("slab", None, "tm"),
        P("slab", None),
        P("slab", None),
    )
    return jax.shard_map(
        on_device, mesh=mesh, in_specs=placed, out_specs=P("slab", None, "tm"), check_vma=False
    )
```

```python
import jax
import jax.numpy as jnp
from jax import lax
from jax.experimental import pallas as pl
from jax.experimental.pallas import tpu as pltpu
from jax.sharding import PartitionSpec as P

MESH = pl.DeviceIdType.MESH
ITERS = 3
SCALE = 32760.0
TINY = 1e-6
PIECES = 4
RUN = 8
DETOUR = (0, 1)
OUT_PIECES = 4


def times_transposed(a, b):
    return lax.dot_general(a, b, (((1,), (1,)), ((), ())), preferred_element_type=jnp.float32)


def body(
    data_ref, tmpl_ref, near_ref, valid_ref, mine_ref, theirs_ref,
    ext, tmpl, near, valid, passing, part, code_out, code_in, norm_out, norm_in, kern, plan,
    local_sem, slab_send, slab_recv, pass_send, pass_recv, code_send, code_recv, norm_send, norm_recv, subj_send, subj_recv,
):
    slab, slabs = lax.axis_index("slab"), lax.axis_size("slab")
    subj, half = lax.axis_index("subj"), lax.axis_index("tm")
    rows, times = data_ref.shape
    width = 128
    blocks = rows // width
    piece = rows // PIECES
    tiles = blocks + PIECES
    has_prev, has_next = slab > 0, slab < slabs - 1
    shared = (slabs // 2 - RUN, slabs // 2 + RUN - 1)
    byway = (shared[0] - RUN, shared[1] + RUN)

    copies = [
        pltpu.make_async_copy(tmpl_ref, tmpl, local_sem.at[0]),
        pltpu.make_async_copy(data_ref, ext.at[pl.ds(0, rows)], local_sem.at[1]),
        pltpu.make_async_copy(near_ref, near, local_sem.at[2]),
        pltpu.make_async_copy(valid_ref, valid, local_sem.at[3]),
    ]
    for copy in copies:
        copy.start()

    barrier = pltpu.get_barrier_semaphore()

    def greet(where):
        pl.semaphore_signal(barrier, inc=1, device_id=where, device_id_type=MESH)

    greet({"subj": 1 - subj})
    greet({"tm": 1 - half})

    @pl.when(has_prev)
    def _():
        greet({"slab": slab - 1})

    @pl.when(has_next)
    def _():
        greet({"slab": slab + 1})

    for crowded, way in zip(shared, byway):

        @pl.when(slab == crowded)
        def _():
            greet({"slab": way, "tm": 1 - half})

        @pl.when(slab == way)
        def _():
            greet({"slab": crowded})

    is_shared = (slab == shared[0]) | (slab == shared[1])
    is_byway = (slab == byway[0]) | (slab == byway[1])

    @pl.when(has_prev & has_next & jnp.logical_not(is_shared | is_byway))
    def _():
        pl.semaphore_wait(barrier, 4)

    @pl.when(is_shared | is_byway)
    def _():
        pl.semaphore_wait(barrier, 5)

    @pl.when(jnp.logical_not(has_prev & has_next))
    def _():
        pl.semaphore_wait(barrier, 3)

    def slab_place(q, up):
        return ext.at[pl.ds(blocks * width + q * 2 * piece + (0 if up else piece), piece)]

    def slab_copy(q, up):
        k = q + (0 if up else PIECES)
        return pltpu.make_async_remote_copy(
            src_ref=data_ref.at[pl.ds(q * piece, piece)],
            dst_ref=slab_place(q, up),
            send_sem=slab_send.at[k],
            recv_sem=slab_recv.at[k],
            device_id={"slab": slab + 1 if up else slab - 1},
            device_id_type=MESH,
        )

    for q in range(PIECES):

        @pl.when(has_next)
        def _():
            slab_copy(q, True).start()

        @pl.when(has_prev)
        def _():
            slab_copy(q, False).start()

    @pl.when(jnp.logical_not(has_prev))
    def _():
        for q in range(PIECES):
            ext[pl.ds(blocks * width + q * 2 * piece, piece), :] = jnp.zeros((piece, times), ext.dtype)

    @pl.when(jnp.logical_not(has_next))
    def _():
        for q in range(PIECES):
            ext[pl.ds(blocks * width + q * 2 * piece + piece, piece), :] = jnp.zeros((piece, times), ext.dtype)

    copies[2].wait()
    copies[3].wait()
    seen = near[...] - (slab - 1) * blocks
    used = valid[...].astype(jnp.float32)
    count = [
        jnp.sum(jnp.where(seen == e, used, 0.0), axis=1, keepdims=True) for e in range(3 * blocks)
    ]
    goal = 1.0 / (width * jnp.sum(used, axis=1, keepdims=True))
    lane = lax.broadcasted_iota(jnp.int32, (1, width), 1)

    def counts(b, tile):
        if tile < blocks:
            return jnp.broadcast_to(count[blocks + tile][b : b + 1], (1, width))
        owner = (tile - blocks) * piece // width
        return jnp.where(lane < piece, count[owner][b : b + 1], count[2 * blocks + owner][b : b + 1])

    eye = lax.broadcasted_iota(jnp.int32, (width, width), 0) == lax.broadcasted_iota(
        jnp.int32, (width, width), 1
    )

    def diagonal(gram, axis):
        return jnp.sum(jnp.where(eye, gram, 0.0), axis=axis, keepdims=True)

    copies[0].wait()
    grams = [
        times_transposed(tmpl[pl.ds(b * width, width), :], tmpl[pl.ds(b * width, width), :])
        for b in range(blocks)
    ]
    row_sq = [diagonal(gram, 1) for gram in grams]
    row_unit = [lax.rsqrt(sq + TINY) * SCALE for sq in row_sq]

    def code_copy(tile):
        return pltpu.make_async_remote_copy(
            src_ref=code_out.at[tile], dst_ref=code_in.at[tile],
            send_sem=code_send.at[tile], recv_sem=code_recv.at[tile],
            device_id={"tm": 1 - half}, device_id_type=MESH,
        )

    def detour_copy(tile, way):
        return pltpu.make_async_remote_copy(
            src_ref=code_out.at[tile], dst_ref=passing.at[tile],
            send_sem=code_send.at[tile], recv_sem=pass_recv.at[tile],
            device_id={"slab": way}, device_id_type=MESH,
        )

    def onward_copy(tile, crowded):
        return pltpu.make_async_remote_copy(
            src_ref=passing.at[tile], dst_ref=code_in.at[tile],
            send_sem=pass_send.at[tile], recv_sem=code_recv.at[tile],
            device_id={"slab": crowded, "tm": 1 - half}, device_id_type=MESH,
        )

    def send_code(tile):
        if tile not in DETOUR:
            code_copy(tile).start()
            return

        @pl.when(jnp.logical_not(is_shared))
        def _():
            code_copy(tile).start()

        for crowded, way in zip(shared, byway):

            @pl.when(slab == crowded)
            def _():
                detour_copy(tile, way).start()

    def pass_on():
        for crowded, way in zip(shared, byway):

            @pl.when(slab == way)
            def _():
                for tile in DETOUR:
                    detour_copy(tile, way).wait_recv()
                    onward_copy(tile, crowded).start()

    def norm_copy(tile):
        return pltpu.make_async_remote_copy(
            src_ref=norm_out.at[tile], dst_ref=norm_in.at[tile],
            send_sem=norm_send.at[tile], recv_sem=norm_recv.at[tile],
            device_id={"tm": 1 - half}, device_id_type=MESH,
        )

    def first_pass(tile):
        data = ext[pl.ds(tile * width, width), :]
        col_sq = diagonal(times_transposed(data, data), 0)
        norm_out[tile] = jnp.concatenate(
            [col_sq] + [diagonal(gram, 0) for gram in grams] + [jnp.zeros((8 - 1 - blocks, width), jnp.float32)], axis=0
        )
        norm_copy(tile).start()
        col_unit = lax.rsqrt(col_sq + TINY)
        for b in range(blocks):
            at = pl.ds(b * width, width)
            cross = times_transposed(tmpl[at, :], data)
            part[tile, at, :] = cross
            code_out[tile, at, :] = jnp.round(cross * row_unit[b] * col_unit).astype(jnp.int32).astype(jnp.int16)
        send_code(tile)

    scales = {}

    def second_pass(tile):
        norm_copy(tile).wait_recv()
        there = norm_in[tile]
        if tile == 0:
            for b in range(blocks):
                other = jnp.sum(jnp.where(eye, there[1 + b : 2 + b], 0.0), axis=1, keepdims=True)
                row_scale = lax.rsqrt(row_sq[b] + other + 1e-6)
                scales[b] = (row_scale, row_scale * ((other + TINY) * lax.rsqrt(other + TINY)))
        col_sq = norm_out[tile][0:1]
        other = there[0:1]
        col_scale = lax.rsqrt(col_sq + other + 1e-6) * (1.0 / 0.03)
        col_other = col_scale * ((other + TINY) * lax.rsqrt(other + TINY)) * (1.0 / SCALE)
        code_copy(tile).wait_recv()
        for b in range(blocks):
            at = pl.ds(b * width, width)
            logits = part[tile, at, :] * (scales[b][0] * col_scale)
            logits += code_in[tile, at, :].astype(jnp.int32).astype(jnp.float32) * (scales[b][1] * col_other)
            kern[tile, at, :] = jnp.exp(logits)

    def arrived(q):
        @pl.when(has_prev)
        def _():
            slab_copy(q, True).wait_recv()

        @pl.when(has_next)
        def _():
            slab_copy(q, False).wait_recv()

    copies[1].wait()
    for tile in range(blocks):
        first_pass(tile)
    pass_on()
    for q in range(PIECES):
        arrived(q)
        first_pass(blocks + q)
    for tile in range(tiles):
        second_pass(tile)

    for b in range(blocks):
        at = pl.ds(b * width, width)
        number = [counts(b, tile) for tile in range(tiles)]
        weight = number
        for _ in range(ITERS):
            total = sum(kern[tile, at, :] * weight[tile] for tile in range(tiles))
            row_weight = (1.0 / width) / jnp.sum(total, axis=1, keepdims=True)
            weight = [
                number[tile] * goal[b : b + 1] / jnp.sum(kern[tile, at, :] * row_weight, axis=0, keepdims=True)
                for tile in range(tiles)
            ]
        total = sum(kern[tile, at, :] * weight[tile] for tile in range(tiles))
        share = 0.5 / jnp.sum(total, axis=1, keepdims=True)
        for tile in range(tiles):
            plan[at, pl.ds(tile * width, width)] = (kern[tile, at, :] * weight[tile] * share).astype(plan.dtype)

    wide = times // OUT_PIECES
    moves = []
    for c in range(OUT_PIECES):
        at = (slice(None), pl.ds(c * wide, wide))
        mine_ref[at] = jnp.dot(plan[...], ext[at], preferred_element_type=jnp.float32).astype(mine_ref.dtype)
        moves.append(
            pltpu.make_async_remote_copy(
                src_ref=mine_ref.at[at], dst_ref=theirs_ref.at[at],
                send_sem=subj_send.at[c], recv_sem=subj_recv.at[c],
                device_id={"subj": 1 - subj}, device_id_type=MESH,
            )
        )
        moves[-1].start()

    @pl.when(is_byway)
    def _():
        for tile in DETOUR:
            onward_copy(tile, slab).wait_send()

    for tile in range(tiles):
        norm_copy(tile).wait_send()
        code_copy(tile).wait_send()
    for q in range(PIECES):

        @pl.when(has_next)
        def _():
            slab_copy(q, True).wait_send()

        @pl.when(has_prev)
        def _():
            slab_copy(q, False).wait_send()

    for move in moves:
        move.wait()


def on_device(subject_data, template, neighbours, valid):
    _, blocks, width, times = subject_data.shape
    rows = blocks * width
    tiles = blocks + PIECES
    dma = pltpu.SemaphoreType.DMA
    hbm = pl.BlockSpec(memory_space=pltpu.HBM)
    vmem = pl.BlockSpec(memory_space=pltpu.VMEM)
    mine, theirs = pl.pallas_call(
        body,
        out_shape=[jax.ShapeDtypeStruct((rows, times), jnp.bfloat16)] * 2,
        in_specs=[hbm] * 4,
        out_specs=[vmem] * 2,
        scratch_shapes=[
            pltpu.VMEM((tiles * width, times), jnp.bfloat16),
            pltpu.VMEM((rows, times), jnp.bfloat16),
            pltpu.VMEM(neighbours.shape, neighbours.dtype),
            pltpu.VMEM(valid.shape, valid.dtype),
            pltpu.VMEM((len(DETOUR), rows, width), jnp.int16),
            pltpu.VMEM((tiles, rows, width), jnp.float32),
            pltpu.VMEM((tiles, rows, width), jnp.int16),
            pltpu.VMEM((tiles, rows, width), jnp.int16),
            pltpu.VMEM((tiles, 8, width), jnp.float32),
            pltpu.VMEM((tiles, 8, width), jnp.float32),
            pltpu.VMEM((tiles, rows, width), jnp.float32),
            pltpu.VMEM((rows, tiles * width), jnp.bfloat16),
            dma((4,)),
            dma((2 * PIECES,)), dma((2 * PIECES,)),
            dma((len(DETOUR),)), dma((len(DETOUR),)),
            dma((tiles,)), dma((tiles,)),
            dma((tiles,)), dma((tiles,)),
            dma((OUT_PIECES,)), dma((OUT_PIECES,)),
        ],
        compiler_params=pltpu.CompilerParams(
            collective_id=0, has_side_effects=True, vmem_limit_bytes=32 * 2**20
        ),
    )(*[pltpu.with_memory_space_constraint(x, pltpu.HBM) for x in (subject_data.reshape(rows, times), template.reshape(rows, times), neighbours, valid)])
    total = mine.astype(jnp.float32) + theirs.astype(jnp.float32)
    return total.astype(jnp.bfloat16).reshape(template.shape)


def solution(mesh):
    placed = (
        P("subj", "slab", None, "tm"),
        P("slab", None, "tm"),
        P("slab", None),
        P("slab", None),
    )
    return jax.shard_map(
        on_device, mesh=mesh, in_specs=placed, out_specs=P("slab", None, "tm"), check_vma=False
    )
```

```python
import jax
import jax.numpy as jnp
from jax import lax
from jax.experimental import pallas as pl
from jax.experimental.pallas import tpu as pltpu
from jax.sharding import PartitionSpec as P

MESH = pl.DeviceIdType.MESH
ITERS = 3
SCALE = 32760.0
TINY = 1e-6
PIECES = (64, 64, 64, 32, 32)
RUN = 8
LOWER_DETOUR = (0, 1, 2, 3)
UPPER_DETOUR = (0, 1)
OUT_PIECES = 4


def times_transposed(a, b):
    return lax.dot_general(a, b, (((1,), (1,)), ((), ())), preferred_element_type=jnp.float32)


def body(
    data_ref, tmpl_ref, near_ref, valid_ref, mine_ref, theirs_ref,
    ext, tmpl, near, valid, passing, part, code_out, code_in, norm_out, norm_in, kern, plan,
    local_sem, slab_send, slab_recv, pass_send, pass_recv, code_send, code_recv, norm_send, norm_recv, subj_send, subj_recv, hello,
):
    slab, slabs = lax.axis_index("slab"), lax.axis_size("slab")
    subj, half = lax.axis_index("subj"), lax.axis_index("tm")
    rows, times = data_ref.shape
    width = 128
    blocks = rows // width
    columns = [width] * blocks + [2 * piece for piece in PIECES]
    tiles = len(columns)
    starts = [sum(columns[:tile]) for tile in range(tiles)]
    has_prev, has_next = slab > 0, slab < slabs - 1
    shared = (slabs // 2 - RUN, slabs // 2 + RUN - 1)
    routes = ((shared[0], 0, LOWER_DETOUR), (shared[1], shared[1] + RUN, UPPER_DETOUR))

    copies = [
        pltpu.make_async_copy(tmpl_ref, tmpl, local_sem.at[0]),
        pltpu.make_async_copy(data_ref, ext.at[pl.ds(0, rows)], local_sem.at[1]),
        pltpu.make_async_copy(near_ref, near, local_sem.at[2]),
        pltpu.make_async_copy(valid_ref, valid, local_sem.at[3]),
    ]
    for copy in copies:
        copy.start()

    barrier = pltpu.get_barrier_semaphore()

    def greet(where):
        pl.semaphore_signal(barrier, inc=1, device_id=where, device_id_type=MESH)

    greet({"subj": 1 - subj})

    @pl.when(half == 0)
    def _():
        greet({"tm": 1})

    @pl.when(has_prev)
    def _():
        greet({"slab": slab - 1})

    @pl.when(has_next)
    def _():
        greet({"slab": slab + 1})

    for crowded, way, _ in routes:

        @pl.when(slab == crowded)
        def _():
            greet({"slab": way, "tm": 1 - half})

        @pl.when(slab == way)
        def _():
            greet({"slab": crowded})

    greeted = (slab == shared[0]) | (slab == shared[1]) | (slab == routes[1][1])

    @pl.when(greeted)
    def _():
        pl.semaphore_wait(barrier, 4 + half)

    @pl.when(slab == slabs - 1)
    def _():
        pl.semaphore_wait(barrier, 2 + half)

    @pl.when(jnp.logical_not(greeted | (slab == slabs - 1)))
    def _():
        pl.semaphore_wait(barrier, 3 + half)

    @pl.when(half == 1)
    def _():
        pl.semaphore_signal(hello, inc=1, device_id={"tm": 0}, device_id_type=MESH)

    def slab_place(q, up):
        return pl.ds(starts[blocks + q] + (0 if up else PIECES[q]), PIECES[q])

    def slab_copy(q, up):
        k = q + (0 if up else len(PIECES))
        return pltpu.make_async_remote_copy(
            src_ref=data_ref.at[pl.ds(sum(PIECES[:q]), PIECES[q])],
            dst_ref=ext.at[slab_place(q, up)],
            send_sem=slab_send.at[k],
            recv_sem=slab_recv.at[k],
            device_id={"slab": slab + 1 if up else slab - 1},
            device_id_type=MESH,
        )

    for q in range(len(PIECES)):

        @pl.when(has_next)
        def _():
            slab_copy(q, True).start()

        @pl.when(has_prev)
        def _():
            slab_copy(q, False).start()

    for there, up in ((has_prev, True), (has_next, False)):

        @pl.when(jnp.logical_not(there))
        def _():
            for q, piece in enumerate(PIECES):
                ext[slab_place(q, up), :] = jnp.zeros((piece, times), ext.dtype)

    norm_out[...] = jnp.zeros(norm_out.shape, norm_out.dtype)

    copies[2].wait()
    copies[3].wait()
    seen = near[...] - (slab - 1) * blocks
    used = valid[...].astype(jnp.float32)
    count = [
        jnp.sum(jnp.where(seen == e, used, 0.0), axis=1, keepdims=True) for e in range(3 * blocks)
    ]
    goal = 1.0 / (width * jnp.sum(used, axis=1, keepdims=True))

    def counts(b, tile):
        if tile < blocks:
            return jnp.broadcast_to(count[blocks + tile][b : b + 1], (1, width))
        piece = PIECES[tile - blocks]
        owner = sum(PIECES[: tile - blocks]) // width
        lane = lax.broadcasted_iota(jnp.int32, (1, 2 * piece), 1)
        return jnp.where(lane < piece, count[owner][b : b + 1], count[2 * blocks + owner][b : b + 1])

    def diagonal(gram, axis):
        row, column = (lax.broadcasted_iota(jnp.int32, gram.shape, dim) for dim in (0, 1))
        return jnp.sum(jnp.where(row == column, gram, 0.0), axis=axis, keepdims=True)

    copies[0].wait()
    grams = [
        times_transposed(tmpl[pl.ds(b * width, width), :], tmpl[pl.ds(b * width, width), :])
        for b in range(blocks)
    ]
    row_sq = [diagonal(gram, 1) for gram in grams]
    row_unit = [lax.rsqrt(sq + TINY) * SCALE for sq in row_sq]

    def coded(tile):
        return pl.ds(0, rows * columns[tile] // width)

    def code_place(tile, b):
        beside = width // columns[tile]
        return (tile, pl.ds(b // beside * width, width), pl.ds(b % beside * columns[tile], columns[tile]))

    def code_copy(tile):
        return pltpu.make_async_remote_copy(
            src_ref=code_out.at[tile, coded(tile)], dst_ref=code_in.at[tile, coded(tile)],
            send_sem=code_send.at[tile], recv_sem=code_recv.at[tile],
            device_id={"tm": 1 - half}, device_id_type=MESH,
        )

    def detour_copy(tile, way):
        return pltpu.make_async_remote_copy(
            src_ref=code_out.at[tile, coded(tile)], dst_ref=passing.at[tile, coded(tile)],
            send_sem=code_send.at[tile], recv_sem=pass_recv.at[tile],
            device_id={"slab": way}, device_id_type=MESH,
        )

    def onward_copy(tile, crowded):
        return pltpu.make_async_remote_copy(
            src_ref=passing.at[tile, coded(tile)], dst_ref=code_in.at[tile, coded(tile)],
            send_sem=pass_send.at[tile], recv_sem=code_recv.at[tile],
            device_id={"slab": crowded, "tm": 1 - half}, device_id_type=MESH,
        )

    def send_code(tile):
        ways = [(crowded, way) for crowded, way, taking in routes if tile in taking]
        direct = jnp.bool_(True)
        for crowded, way in ways:
            direct &= slab != crowded

            @pl.when(slab == crowded)
            def _():
                detour_copy(tile, way).start()

        if not ways:
            code_copy(tile).start()
            return

        @pl.when(direct)
        def _():
            code_copy(tile).start()

    def pass_on(route, turn):
        for crowded, way, taking in routes[route : route + 1]:

            @pl.when(slab == way)
            def _():
                for tile in turn:
                    if tile in taking:
                        detour_copy(tile, way).wait_recv()
                        onward_copy(tile, crowded).start()

    def norm_copy(tile):
        return pltpu.make_async_remote_copy(
            src_ref=norm_out.at[tile], dst_ref=norm_in.at[tile],
            send_sem=norm_send.at[tile], recv_sem=norm_recv.at[tile],
            device_id={"tm": 1 - half}, device_id_type=MESH,
        )

    def first_pass(tile):
        data = ext[pl.ds(starts[tile], columns[tile]), :]
        wide = pl.ds(0, columns[tile])
        col_sq = diagonal(times_transposed(data, data), 0)
        norm_out[tile, 0:1, wide] = col_sq
        if tile == 0:
            for b in range(blocks):
                norm_out[tile, 1 + b : 2 + b, :] = diagonal(grams[b], 0)
        col_unit = lax.rsqrt(col_sq + TINY)
        for b in range(blocks):
            at = pl.ds(b * width, width)
            cross = times_transposed(tmpl[at, :], data)
            part[tile, at, wide] = cross
            code_out[code_place(tile, b)] = jnp.round(cross * row_unit[b] * col_unit).astype(jnp.int32).astype(jnp.int16)

    def send(tile):
        norm_copy(tile).start()
        send_code(tile)

    scales = {}

    def second_pass(tile):
        norm_copy(tile).wait_recv()
        wide = pl.ds(0, columns[tile])
        if tile == 0:
            for b in range(blocks):
                row, column = (lax.broadcasted_iota(jnp.int32, (width, width), dim) for dim in (0, 1))
                other = jnp.sum(
                    jnp.where(row == column, norm_in[tile, 1 + b : 2 + b, :], 0.0), axis=1, keepdims=True
                )
                row_scale = lax.rsqrt(row_sq[b] + other + 1e-6)
                scales[b] = (row_scale, row_scale * ((other + TINY) * lax.rsqrt(other + TINY)))
        col_sq = norm_out[tile, 0:1, wide]
        other = norm_in[tile, 0:1, wide]
        col_scale = lax.rsqrt(col_sq + other + 1e-6) * (1.0 / 0.03)
        col_other = col_scale * ((other + TINY) * lax.rsqrt(other + TINY)) * (1.0 / SCALE)
        code_copy(tile).wait_recv()
        for b in range(blocks):
            at = pl.ds(b * width, width)
            logits = part[tile, at, wide] * (scales[b][0] * col_scale)
            logits += code_in[code_place(tile, b)].astype(jnp.int32).astype(jnp.float32) * (scales[b][1] * col_other)
            kern[tile, at, wide] = jnp.exp(logits)

    def arrived(q):
        @pl.when(has_prev)
        def _():
            slab_copy(q, True).wait_recv()

        @pl.when(has_next)
        def _():
            slab_copy(q, False).wait_recv()

    copies[1].wait()
    for tile in range(blocks):
        first_pass(tile)

    @pl.when(half == 0)
    def _():
        pl.semaphore_wait(hello, 1)

    for tile in range(blocks):
        send(tile)
    pass_on(1, UPPER_DETOUR)
    for q in range(len(PIECES)):
        arrived(q)
        first_pass(blocks + q)
        send(blocks + q)
        if q == 1:
            pass_on(0, [tile for tile in LOWER_DETOUR if tile < blocks])
    pass_on(0, [tile for tile in LOWER_DETOUR if tile >= blocks])
    for tile in range(tiles):
        second_pass(tile)

    for b in range(blocks):
        at = pl.ds(b * width, width)
        number = [counts(b, tile) for tile in range(tiles)]
        weight = number

        def flow(tile, w):
            return kern[tile, at, pl.ds(0, columns[tile])] * w

        def row_sums(weight):
            whole = sum(flow(tile, weight[tile]) for tile in range(tiles) if columns[tile] == width)
            sums = jnp.sum(whole, axis=1, keepdims=True)
            rest = [flow(tile, weight[tile]) for tile in range(tiles) if columns[tile] < width]
            return sums + jnp.sum(sum(rest), axis=1, keepdims=True) if rest else sums

        for _ in range(ITERS):
            row_weight = (1.0 / width) / row_sums(weight)
            weight = [
                number[tile] * goal[b : b + 1] / jnp.sum(flow(tile, row_weight), axis=0, keepdims=True)
                for tile in range(tiles)
            ]
        share = 0.5 / row_sums(weight)
        for tile in range(tiles):
            plan[at, pl.ds(starts[tile], columns[tile])] = (flow(tile, weight[tile]) * share).astype(plan.dtype)

    wide = times // OUT_PIECES
    moves = []
    for c in range(OUT_PIECES):
        at = (slice(None), pl.ds(c * wide, wide))
        mine_ref[at] = jnp.dot(plan[...], ext[at], preferred_element_type=jnp.float32).astype(mine_ref.dtype)
        moves.append(
            pltpu.make_async_remote_copy(
                src_ref=mine_ref.at[at], dst_ref=theirs_ref.at[at],
                send_sem=subj_send.at[c], recv_sem=subj_recv.at[c],
                device_id={"subj": 1 - subj}, device_id_type=MESH,
            )
        )
        moves[-1].start()

    for crowded, way, taking in routes:

        @pl.when(slab == way)
        def _():
            for tile in taking:
                onward_copy(tile, crowded).wait_send()

    for tile in range(tiles):
        norm_copy(tile).wait_send()
        code_copy(tile).wait_send()
    for q in range(len(PIECES)):

        @pl.when(has_next)
        def _():
            slab_copy(q, True).wait_send()

        @pl.when(has_prev)
        def _():
            slab_copy(q, False).wait_send()

    for move in moves:
        move.wait()


def on_device(subject_data, template, neighbours, valid):
    _, blocks, width, times = subject_data.shape
    rows = blocks * width
    pieces, tiles = len(PIECES), blocks + len(PIECES)
    detours = max(LOWER_DETOUR + UPPER_DETOUR) + 1
    dma = pltpu.SemaphoreType.DMA
    hbm = pl.BlockSpec(memory_space=pltpu.HBM)
    vmem = pl.BlockSpec(memory_space=pltpu.VMEM)
    mine, theirs = pl.pallas_call(
        body,
        out_shape=[jax.ShapeDtypeStruct((rows, times), jnp.bfloat16)] * 2,
        in_specs=[hbm] * 4,
        out_specs=[vmem] * 2,
        scratch_shapes=[
            pltpu.VMEM((3 * rows, times), jnp.bfloat16),
            pltpu.VMEM((rows, times), jnp.bfloat16),
            pltpu.VMEM(neighbours.shape, neighbours.dtype),
            pltpu.VMEM(valid.shape, valid.dtype),
            pltpu.VMEM((detours, rows, width), jnp.int16),
            pltpu.VMEM((tiles, rows, width), jnp.float32),
            pltpu.VMEM((tiles, rows, width), jnp.int16),
            pltpu.VMEM((tiles, rows, width), jnp.int16),
            pltpu.VMEM((tiles, 8, width), jnp.float32),
            pltpu.VMEM((tiles, 8, width), jnp.float32),
            pltpu.VMEM((tiles, rows, width), jnp.float32),
            pltpu.VMEM((rows, 3 * rows), jnp.bfloat16),
            dma((4,)),
            dma((2 * pieces,)), dma((2 * pieces,)),
            dma((detours,)), dma((detours,)),
            dma((tiles,)), dma((tiles,)),
            dma((tiles,)), dma((tiles,)),
            dma((OUT_PIECES,)), dma((OUT_PIECES,)),
            pltpu.SemaphoreType.REGULAR,
        ],
        compiler_params=pltpu.CompilerParams(
            collective_id=0, has_side_effects=True, vmem_limit_bytes=32 * 2**20
        ),
    )(*[pltpu.with_memory_space_constraint(x, pltpu.HBM) for x in (subject_data.reshape(rows, times), template.reshape(rows, times), neighbours, valid)])
    total = mine.astype(jnp.float32) + theirs.astype(jnp.float32)
    return total.astype(jnp.bfloat16).reshape(template.shape)


def solution(mesh):
    placed = (
        P("subj", "slab", None, "tm"),
        P("slab", None, "tm"),
        P("slab", None),
        P("slab", None),
    )
    return jax.shard_map(
        on_device, mesh=mesh, in_specs=placed, out_specs=P("slab", None, "tm"), check_vma=False
    )
```

```python
import jax
import jax.numpy as jnp
from jax import lax
from jax.experimental import pallas as pl
from jax.experimental.pallas import tpu as pltpu
from jax.sharding import PartitionSpec as P

MESH = pl.DeviceIdType.MESH
ITERS = 3
SCALE = 32760.0
TINY = 1e-6
PIECES = (64, 64, 64, 32, 32)
RUN = 8
DETOUR = (0, 1, 2)
OUT_PIECES = 2


def times_transposed(a, b):
    return lax.dot_general(a, b, (((1,), (1,)), ((), ())), preferred_element_type=jnp.float32)


def body(
    data_ref, tmpl_ref, near_ref, valid_ref, mine_ref, theirs_ref,
    ext, tmpl, near, valid, passing, part, code_out, code_in, norm_out, norm_in, kern, plan,
    local_sem, slab_send, slab_recv, pass_send, pass_recv, code_send, code_recv, norm_send, norm_recv, subj_send, subj_recv, hello,
):
    slab, slabs = lax.axis_index("slab"), lax.axis_size("slab")
    subj, half = lax.axis_index("subj"), lax.axis_index("tm")
    rows, times = data_ref.shape
    width = 128
    blocks = rows // width
    columns = [width] * blocks + [2 * piece for piece in PIECES]
    tiles = len(columns)
    starts = [sum(columns[:tile]) for tile in range(tiles)]
    has_prev, has_next = slab > 0, slab < slabs - 1
    lower, upper = routes = ((slabs // 2 - RUN, 0), (slabs // 2 + RUN - 1, slabs - 1))

    copies = [
        pltpu.make_async_copy(tmpl_ref, tmpl, local_sem.at[0]),
        pltpu.make_async_copy(data_ref, ext.at[pl.ds(0, rows)], local_sem.at[1]),
        pltpu.make_async_copy(near_ref, near, local_sem.at[2]),
        pltpu.make_async_copy(valid_ref, valid, local_sem.at[3]),
    ]
    for copy in copies:
        copy.start()

    barrier = pltpu.get_barrier_semaphore()

    def greet(where):
        pl.semaphore_signal(barrier, inc=1, device_id=where, device_id_type=MESH)

    @pl.when(subj == 1)
    def _():
        greet({"subj": 0})

    @pl.when(half == 0)
    def _():
        greet({"tm": 1})

    @pl.when(has_prev)
    def _():
        greet({"slab": slab - 1})

    @pl.when(slab == lower[0])
    def _():
        greet({"slab": lower[1], "tm": 1 - half})

    @pl.when(slab == lower[1])
    def _():
        greet({"slab": lower[0]})

    @pl.when(slab == upper[0])
    def _():
        greet({"slab": upper[1]})
        greet({"slab": upper[1], "tm": 1 - half})

    on_lower = (slab == lower[0]) | (slab == lower[1])

    @pl.when(on_lower)
    def _():
        pl.semaphore_wait(barrier, 3 - subj + half)

    @pl.when(slab == upper[1])
    def _():
        pl.semaphore_wait(barrier, 3 - subj + half)

    @pl.when(jnp.logical_not(on_lower | (slab == upper[1])))
    def _():
        pl.semaphore_wait(barrier, 2 - subj + half)

    def hail(k, where):
        pl.semaphore_signal(hello.at[k], inc=1, device_id=where, device_id_type=MESH)

    @pl.when(has_next)
    def _():
        hail(0, {"slab": slab + 1})

    @pl.when(subj == 0)
    def _():
        hail(1, {"subj": 1})

    @pl.when(half == 1)
    def _():
        hail(2, {"tm": 0})

    @pl.when(slab == upper[1])
    def _():
        hail(3, {"slab": upper[0]})

    def slab_place(q, up):
        return pl.ds(starts[blocks + q] + (0 if up else PIECES[q]), PIECES[q])

    def slab_copy(q, up):
        k = q + (0 if up else len(PIECES))
        return pltpu.make_async_remote_copy(
            src_ref=data_ref.at[pl.ds(sum(PIECES[:q]), PIECES[q])],
            dst_ref=ext.at[slab_place(q, up)],
            send_sem=slab_send.at[k],
            recv_sem=slab_recv.at[k],
            device_id={"slab": slab + 1 if up else slab - 1},
            device_id_type=MESH,
        )

    for q in range(len(PIECES)):

        @pl.when(has_next)
        def _():
            slab_copy(q, True).start()

    for there, up in ((has_prev, True), (has_next, False)):

        @pl.when(jnp.logical_not(there))
        def _():
            for q, piece in enumerate(PIECES):
                ext[slab_place(q, up), :] = jnp.zeros((piece, times), ext.dtype)

    norm_out[...] = jnp.zeros(norm_out.shape, norm_out.dtype)

    copies[2].wait()
    copies[3].wait()
    seen = near[...] - (slab - 1) * blocks
    used = valid[...].astype(jnp.float32)
    count = [
        jnp.sum(jnp.where(seen == e, used, 0.0), axis=1, keepdims=True) for e in range(3 * blocks)
    ]
    goal = 1.0 / (width * jnp.sum(used, axis=1, keepdims=True))

    def counts(b, tile):
        if tile < blocks:
            return jnp.broadcast_to(count[blocks + tile][b : b + 1], (1, width))
        piece = PIECES[tile - blocks]
        owner = sum(PIECES[: tile - blocks]) // width
        lane = lax.broadcasted_iota(jnp.int32, (1, 2 * piece), 1)
        return jnp.where(lane < piece, count[owner][b : b + 1], count[2 * blocks + owner][b : b + 1])

    def diagonal(gram, axis):
        row, column = (lax.broadcasted_iota(jnp.int32, gram.shape, dim) for dim in (0, 1))
        return jnp.sum(jnp.where(row == column, gram, 0.0), axis=axis, keepdims=True)

    copies[0].wait()
    grams = [
        times_transposed(tmpl[pl.ds(b * width, width), :], tmpl[pl.ds(b * width, width), :])
        for b in range(blocks)
    ]
    row_sq = [diagonal(gram, 1) for gram in grams]
    row_unit = [lax.rsqrt(sq + TINY) * SCALE for sq in row_sq]

    def coded(tile):
        return pl.ds(0, rows * columns[tile] // width)

    def code_place(tile, b):
        beside = width // columns[tile]
        return (tile, pl.ds(b // beside * width, width), pl.ds(b % beside * columns[tile], columns[tile]))

    def code_copy(tile):
        return pltpu.make_async_remote_copy(
            src_ref=code_out.at[tile, coded(tile)], dst_ref=code_in.at[tile, coded(tile)],
            send_sem=code_send.at[tile], recv_sem=code_recv.at[tile],
            device_id={"tm": 1 - half}, device_id_type=MESH,
        )

    def detour_copy(tile, way):
        return pltpu.make_async_remote_copy(
            src_ref=code_out.at[tile, coded(tile)], dst_ref=passing.at[tile, coded(tile)],
            send_sem=code_send.at[tile], recv_sem=pass_recv.at[tile],
            device_id={"slab": way}, device_id_type=MESH,
        )

    def onward_copy(tile, crowded):
        return pltpu.make_async_remote_copy(
            src_ref=passing.at[tile, coded(tile)], dst_ref=code_in.at[tile, coded(tile)],
            send_sem=pass_send.at[tile], recv_sem=code_recv.at[tile],
            device_id={"slab": crowded, "tm": 1 - half}, device_id_type=MESH,
        )

    def send_code(tile):
        if tile not in DETOUR:
            code_copy(tile).start()
            return

        for crowded, way in routes:

            @pl.when(slab == crowded)
            def _():
                detour_copy(tile, way).start()

        @pl.when((slab != lower[0]) & (slab != upper[0]))
        def _():
            code_copy(tile).start()

    def pass_on(turn):
        for crowded, way in routes:

            @pl.when(slab == way)
            def _():
                for tile in turn:
                    detour_copy(tile, way).wait_recv()
                    onward_copy(tile, crowded).start()

    def norm_copy(tile):
        return pltpu.make_async_remote_copy(
            src_ref=norm_out.at[tile], dst_ref=norm_in.at[tile],
            send_sem=norm_send.at[tile], recv_sem=norm_recv.at[tile],
            device_id={"tm": 1 - half}, device_id_type=MESH,
        )

    def first_pass(tile):
        data = ext[pl.ds(starts[tile], columns[tile]), :]
        wide = pl.ds(0, columns[tile])
        col_sq = diagonal(times_transposed(data, data), 0)
        norm_out[tile, 0:1, wide] = col_sq
        if tile == 0:
            for b in range(blocks):
                norm_out[tile, 1 + b : 2 + b, :] = diagonal(grams[b], 0)
        col_unit = lax.rsqrt(col_sq + TINY)
        for b in range(blocks):
            at = pl.ds(b * width, width)
            cross = times_transposed(tmpl[at, :], data)
            part[tile, at, wide] = cross
            code_out[code_place(tile, b)] = jnp.round(cross * row_unit[b] * col_unit).astype(jnp.int32).astype(jnp.int16)

    def send(tile):
        norm_copy(tile).start()
        send_code(tile)

    scales = {}

    def second_pass(tile):
        norm_copy(tile).wait_recv()
        wide = pl.ds(0, columns[tile])
        if tile == 0:
            for b in range(blocks):
                row, column = (lax.broadcasted_iota(jnp.int32, (width, width), dim) for dim in (0, 1))
                other = jnp.sum(
                    jnp.where(row == column, norm_in[tile, 1 + b : 2 + b, :], 0.0), axis=1, keepdims=True
                )
                row_scale = lax.rsqrt(row_sq[b] + other + 1e-6)
                scales[b] = (row_scale, row_scale * ((other + TINY) * lax.rsqrt(other + TINY)))
        col_sq = norm_out[tile, 0:1, wide]
        other = norm_in[tile, 0:1, wide]
        col_scale = lax.rsqrt(col_sq + other + 1e-6) * (1.0 / 0.03)
        col_other = col_scale * ((other + TINY) * lax.rsqrt(other + TINY)) * (1.0 / SCALE)
        code_copy(tile).wait_recv()
        for b in range(blocks):
            at = pl.ds(b * width, width)
            logits = part[tile, at, wide] * (scales[b][0] * col_scale)
            logits += code_in[code_place(tile, b)].astype(jnp.int32).astype(jnp.float32) * (scales[b][1] * col_other)
            kern[tile, at, wide] = jnp.exp(logits)

    def arrived(q):
        @pl.when(has_prev)
        def _():
            slab_copy(q, True).wait_recv()

        @pl.when(has_next)
        def _():
            slab_copy(q, False).wait_recv()

    copies[1].wait()
    for tile in range(blocks):
        first_pass(tile)

    @pl.when(has_prev)
    def _():
        pl.semaphore_wait(hello.at[0], 1)
        for q in range(len(PIECES)):
            slab_copy(q, False).start()

    @pl.when(half == 0)
    def _():
        pl.semaphore_wait(hello.at[2], 1)

    @pl.when(slab == upper[0])
    def _():
        pl.semaphore_wait(hello.at[3], 1)

    for tile in range(blocks):
        send(tile)
    for q in range(len(PIECES)):
        arrived(q)
        first_pass(blocks + q)
        send(blocks + q)
        if q == 1:
            pass_on([tile for tile in DETOUR if tile < blocks])
    pass_on([tile for tile in DETOUR if tile >= blocks])
    for tile in range(tiles):
        second_pass(tile)

    for b in range(blocks):
        at = pl.ds(b * width, width)
        number = [counts(b, tile) for tile in range(tiles)]
        weight = number

        def flow(tile, w):
            return kern[tile, at, pl.ds(0, columns[tile])] * w

        def row_sums(weight):
            whole = sum(flow(tile, weight[tile]) for tile in range(tiles) if columns[tile] == width)
            sums = jnp.sum(whole, axis=1, keepdims=True)
            rest = [flow(tile, weight[tile]) for tile in range(tiles) if columns[tile] < width]
            return sums + jnp.sum(sum(rest), axis=1, keepdims=True) if rest else sums

        for _ in range(ITERS):
            row_weight = (1.0 / width) / row_sums(weight)
            weight = [
                number[tile] * goal[b : b + 1] / jnp.sum(flow(tile, row_weight), axis=0, keepdims=True)
                for tile in range(tiles)
            ]
        share = 0.5 / row_sums(weight)
        for tile in range(tiles):
            plan[at, pl.ds(starts[tile], columns[tile])] = (flow(tile, weight[tile]) * share).astype(plan.dtype)

    @pl.when(subj == 1)
    def _():
        pl.semaphore_wait(hello.at[1], 1)

    wide = times // OUT_PIECES
    moves = []
    for c in range(OUT_PIECES):
        at = (slice(None), pl.ds(c * wide, wide))
        mine_ref[at] = jnp.dot(plan[...], ext[at], preferred_element_type=jnp.float32).astype(mine_ref.dtype)
        moves.append(
            pltpu.make_async_remote_copy(
                src_ref=mine_ref.at[at], dst_ref=theirs_ref.at[at],
                send_sem=subj_send.at[c], recv_sem=subj_recv.at[c],
                device_id={"subj": 1 - subj}, device_id_type=MESH,
            )
        )
        moves[-1].start()

    for crowded, way in routes:

        @pl.when(slab == way)
        def _():
            for tile in DETOUR:
                onward_copy(tile, crowded).wait_send()

    for tile in range(tiles):
        norm_copy(tile).wait_send()
        code_copy(tile).wait_send()
    for q in range(len(PIECES)):

        @pl.when(has_next)
        def _():
            slab_copy(q, True).wait_send()

        @pl.when(has_prev)
        def _():
            slab_copy(q, False).wait_send()

    for move in moves:
        move.wait()


def on_device(subject_data, template, neighbours, valid):
    _, blocks, width, times = subject_data.shape
    rows = blocks * width
    pieces, tiles = len(PIECES), blocks + len(PIECES)
    detours = len(DETOUR)
    dma = pltpu.SemaphoreType.DMA
    hbm = pl.BlockSpec(memory_space=pltpu.HBM)
    vmem = pl.BlockSpec(memory_space=pltpu.VMEM)
    mine, theirs = pl.pallas_call(
        body,
        out_shape=[jax.ShapeDtypeStruct((rows, times), jnp.bfloat16)] * 2,
        in_specs=[hbm] * 4,
        out_specs=[vmem] * 2,
        scratch_shapes=[
            pltpu.VMEM((3 * rows, times), jnp.bfloat16),
            pltpu.VMEM((rows, times), jnp.bfloat16),
            pltpu.VMEM(neighbours.shape, neighbours.dtype),
            pltpu.VMEM(valid.shape, valid.dtype),
            pltpu.VMEM((detours, rows, width), jnp.int16),
            pltpu.VMEM((tiles, rows, width), jnp.float32),
            pltpu.VMEM((tiles, rows, width), jnp.int16),
            pltpu.VMEM((tiles, rows, width), jnp.int16),
            pltpu.VMEM((tiles, 8, width), jnp.float32),
            pltpu.VMEM((tiles, 8, width), jnp.float32),
            pltpu.VMEM((tiles, rows, width), jnp.float32),
            pltpu.VMEM((rows, 3 * rows), jnp.bfloat16),
            dma((4,)),
            dma((2 * pieces,)), dma((2 * pieces,)),
            dma((detours,)), dma((detours,)),
            dma((tiles,)), dma((tiles,)),
            dma((tiles,)), dma((tiles,)),
            dma((OUT_PIECES,)), dma((OUT_PIECES,)),
            pltpu.SemaphoreType.REGULAR((4,)),
        ],
        compiler_params=pltpu.CompilerParams(
            collective_id=0, has_side_effects=True, vmem_limit_bytes=32 * 2**20
        ),
    )(*[pltpu.with_memory_space_constraint(x, pltpu.HBM) for x in (subject_data.reshape(rows, times), template.reshape(rows, times), neighbours, valid)])
    total = mine.astype(jnp.float32) + theirs.astype(jnp.float32)
    return total.astype(jnp.bfloat16).reshape(template.shape)


def solution(mesh):
    placed = (
        P("subj", "slab", None, "tm"),
        P("slab", None, "tm"),
        P("slab", None),
        P("slab", None),
    )
    return jax.shard_map(
        on_device, mesh=mesh, in_specs=placed, out_specs=P("slab", None, "tm"), check_vma=False
    )
```
